32 devices in a mesh: wide: 8 (over y, x, core), narrow: 4 (over z).
Axes of the slice: x: 2, y: 2, z: 4, core: 2. Of those that a mesh axis runs over, the one named last changes fastest.
Arguments:
- amps: float32 [1, 16, 640, 640], P(None, 'wide', 'narrow'), may hold values from -6 to 6
- cycle: float32 [16, 640, 5120], P(None, 'wide', 'narrow'), may hold values from -0.25 to 0.25
- irrep_i: int32 [1], replicated, may hold values from 0 to 7
- irrep_k: int32 [16], replicated, may hold values from 0 to 7, as said below
- irrep_j: int32 [8], replicated, may hold values from 0 to 7, as said below
- irrep_v: int32 [640], replicated, may hold values from 0 to 7, as said below
Outputs:
- cycle_term: float32 [1, 8, 640, 640], P(None, 'wide', 'narrow')
The draws below stay inside these ranges and needn't reach their ends.
Inputs may be any that keep to these rules, and one draw needn't show every extreme that they name: `irrep_k`: nondecreasing along the orbitals, the first 0 and the last 7. `irrep_j`: nondecreasing along the orbitals, the first 0 and the last 7. `irrep_v`: nondecreasing along the orbitals, the first 0 and the last 7.
All inputs are finite; a program needn't handle non-finite values.
Results may differ from the reference program's by a relative error of at most 0.000071.
Values sent between devices are 32-bit elements; how exact they have to be, the bound alone decides.
A program may use at most 64 MiB of HBM per device.

```python
import jax
import jax.numpy as jnp
from jax import lax

V = 640
OI = 1
OK = 16
OJ = 8


def sorted_labels(key, count):
    cuts = jnp.sort(jax.random.randint(key, (7,), 1, count))
    places = jnp.arange(count)
    return jnp.sum((places[:, None] >= cuts[None, :]).astype(jnp.int32), axis=1).astype(jnp.int32)


def draw_irrep_k(key, part):
    return sorted_labels(jax.random.fold_in(key, 11), OK)


def draw_irrep_j(key, part):
    return sorted_labels(jax.random.fold_in(key, 23), OJ)


def draw_irrep_v(key, part):
    return sorted_labels(jax.random.fold_in(key, 37), V)


def with_spikes(result, key, source, target, blocks, factor):
    def block_of(dim):
        return (jnp.arange(result.shape[dim]) // (result.shape[dim] // blocks)).reshape((-1,) + (1,) * (result.ndim - 1 - dim))

    near = jax.random.permutation(key, blocks)[block_of(target)]
    second = (block_of(target) + blocks // 2) % blocks
    return jnp.where((block_of(source) == near) | (block_of(source) == second), factor * result, result)


def block_scale(stream_key, shape, split, smallest, largest):
    loudness, own = 1.0, jax.random.fold_in(stream_key, 6)
    for axis_at, shards_of in split:
        draws = jnp.exp(jax.random.uniform(jax.random.fold_in(own, axis_at), (shards_of,), jnp.float32, smallest / len(split), largest / len(split)))
        loudness = loudness * jnp.repeat(draws, shape[axis_at] // shards_of).reshape([-1 if axis == axis_at else 1 for axis in range(len(shape))])
    return loudness


def centred(own_key, extent, deviation, most, pieces=(), dtype=jnp.bfloat16):
    gain = block_scale(own_key, extent, pieces, -0.22, 0.18) if pieces else 1.0
    drawn = jax.random.normal(own_key, extent, jnp.float32) * deviation * gain
    return jnp.minimum(jnp.maximum(drawn, -most), most).astype(dtype)


def bell_draw_with(own_key, shape, spread, limit, cuts, heavy, kind=jnp.bfloat16):
    entries = spread * jax.random.normal(own_key, shape, jnp.float32)
    if cuts:
        entries = entries * block_scale(own_key, shape, cuts, -0.22, 0.18)
    return jnp.clip(with_spikes(entries, jax.random.fold_in(own_key, 3), *heavy), -limit, limit).astype(kind)


def setup_inputs(seed: int = 0) -> dict:
    streams_of = jax.random.split(jax.random.key(seed), 7)
    amps = centred(streams_of[0], (OI, OK, V, V), 1.0, 6.0, ((1, 8), (2, 4)), jnp.float32)
    cycle = bell_draw_with(streams_of[1], (OK, V, V * OJ), (OK * V // 8) ** -0.5, 0.25, ((1, 8), (2, 4)), (1, 2, 8, 2.0), jnp.float32)
    irrep_i = jax.random.randint(streams_of[2], (OI,), 0, 8).astype(jnp.int32)
    irrep_k = draw_irrep_k(jax.random.fold_in(streams_of[6], 71), 0)
    irrep_j = draw_irrep_j(jax.random.fold_in(streams_of[6], 71), 0)
    irrep_v = draw_irrep_v(jax.random.fold_in(streams_of[6], 71), 0)
    return dict(amps=amps, cycle=cycle, irrep_i=irrep_i, irrep_k=irrep_k, irrep_j=irrep_j, irrep_v=irrep_v)


def reference(amps, cycle, irrep_i, irrep_k, irrep_j, irrep_v):
    cycle_full = cycle.reshape(OK, V, V, OJ)
    allowed_in = (irrep_i[:, None, None, None] ^ irrep_k[None, :, None, None] ^ irrep_v[None, None, :, None] ^ irrep_v[None, None, None, :]) == 0
    masked = jnp.where(allowed_in, amps, jnp.zeros_like(amps))
    product = jnp.einsum("ikac,kcbj->ijab", masked, cycle_full, precision=lax.Precision.HIGHEST)
    allowed_out = (irrep_i[:, None, None, None] ^ irrep_j[None, :, None, None] ^ irrep_v[None, None, :, None] ^ irrep_v[None, None, None, :]) == 0
    return jnp.where(allowed_out, product, jnp.zeros_like(product))
```

```python
import functools

import jax
import jax.numpy as jnp
from jax import lax
from jax.experimental import pallas as pl
from jax.experimental.pallas import tpu as pltpu
from jax.sharding import PartitionSpec as P

F32 = jnp.float32
BF16 = jnp.bfloat16
MESH = pl.DeviceIdType.MESH


def pick(position, table):
    value = jnp.int32(table[0])
    for place in range(1, len(table)):
        value = jnp.where(position == place, jnp.int32(table[place]), value)
    return value


def near_first(count):
    return [sorted(range(count), key=lambda n: (abs(n - m), n)) for m in range(count)]


def cycle_kernel(ranks, wn, nn, amps, cycle, ir_i, ir_k, ir_j, iv_col, iv_row, out,
                 cyc, cth, ctl, amt, recv_one, xk, yb, yr, xh, xl, acc, send_a, recv_a, send_b, recv_b,
                 send_c, recv_c, out_t,
                 cyc_sem, s1, r1, sl, sr, ry, sa, ra, sb, rb, sc, rc):
    w = lax.axis_index("wide")
    m = lax.axis_index("narrow")
    kl, al, vt = amps.shape
    kt, cl, bj = cycle.shape
    jt = wn
    bl = bj // jt
    depth = kt * cl
    quarter = bl // 4
    pairs = wn // 2
    core = lax.rem(w, 2)
    chip = w // 2
    partner = w + 1 - 2 * core

    load = pltpu.make_async_copy(cycle, cyc, cyc_sem)
    load.start()

    barrier = pltpu.get_barrier_semaphore()
    for d in range(1, wn):
        pl.semaphore_signal(barrier, inc=1, device_id={"wide": lax.rem(w + d, wn)}, device_id_type=MESH)
    for d in range(1, nn):
        pl.semaphore_signal(barrier, inc=1, device_id={"narrow": lax.rem(m + d, nn)}, device_id_type=MESH)

    label_i = ir_i[0]
    ca = iv_col[...] ^ iv_row[m]
    for e in range(kl):
        turned = jnp.transpose(amps[e], (1, 0))
        kept = jnp.where(ca == (label_i ^ ir_k[w * kl + e]), turned, 0.0)
        amt[:, e * al:(e + 1) * al] = kept

    pl.semaphore_wait(barrier, wn + nn - 2)

    first = []
    for d in range(1, wn):
        peer = lax.rem(w + d, wn)
        copy = pltpu.make_async_remote_copy(
            src_ref=amt.at[pl.ds(pl.multiple_of(peer * cl, 8), cl)], dst_ref=recv_one.at[w],
            send_sem=s1.at[d], recv_sem=r1.at[d], device_id={"wide": peer}, device_id_type=MESH)
        copy.start()
        first.append(copy)
    recv_one[w] = amt[pl.ds(pl.multiple_of(w * cl, 8), cl), :]

    if xh.shape[1] > al:
        xh[:, al:] = jnp.zeros((depth, xh.shape[1] - al), BF16)
        xl[:, al:] = jnp.zeros((depth, xh.shape[1] - al), BF16)
    load.wait()
    cyc_rows = cyc.reshape(depth, bj)

    @pl.loop(0, depth // 128)
    def _(row):
        here = pl.multiple_of(row * 128, 128)
        for col in range(bj // 128):
            block = jnp.transpose(cyc_rows[pl.ds(here, 128), col * 128:(col + 1) * 128], (1, 0))
            high = block.astype(BF16)
            cth[col * 128:(col + 1) * 128, pl.ds(here, 128)] = high
            ctl[col * 128:(col + 1) * 128, pl.ds(here, 128)] = (block - high.astype(F32)).astype(BF16)

    for copy in first:
        copy.wait()
    for src in range(wn):
        for e in range(kl):
            xk[src * kl + e] = recv_one[src, :, e * al:(e + 1) * al]

    starts, counts = [], []
    labels = [ir_k[k] for k in range(kt)]
    for g in range(8):
        below = jnp.int32(0)
        same = jnp.int32(0)
        for k in range(kt):
            below = below + jnp.where(labels[k] < g, 1, 0)
            same = same + jnp.where(labels[k] == g, 1, 0)
        starts.append(below)
        counts.append(same)
    for r in range(ranks):
        total = jnp.zeros((cl, al), F32)
        for g in range(8):
            value = xk[jnp.minimum(starts[g] + r, kt - 1)]
            total = total + jnp.where(r < counts[g], value, 0.0)
        yr[r] = total
    yb[m] = jnp.concatenate([yr[r] for r in range(ranks)], axis=1)
    rank_of = []
    for k in range(kt):
        place = jnp.int32(0)
        for other in range(k):
            place = place + jnp.where(labels[other] == labels[k], 1, 0)
        rank_of.append(jnp.minimum(place, ranks - 1))

    def send_right(block):
        return pltpu.make_async_remote_copy(
            src_ref=yb.at[block], dst_ref=yb.at[block], send_sem=sr.at[block], recv_sem=ry.at[block],
            device_id={"narrow": jnp.minimum(m + 1, nn - 1)}, device_id_type=MESH)

    def send_left(block):
        return pltpu.make_async_remote_copy(
            src_ref=yb.at[block], dst_ref=yb.at[block], send_sem=sl.at[block], recv_sem=ry.at[block],
            device_id={"narrow": jnp.maximum(m - 1, 0)}, device_id_type=MESH)

    @pl.when(m < nn - 1)
    def _():
        send_right(m).start()

    @pl.when(m > 0)
    def _():
        send_left(m).start()

    order = near_first(nn)
    blocks = [pick(m, [order[z][t] for z in range(nn)]) for t in range(nn)]
    c_labels = iv_col[pl.ds(pl.multiple_of(w * cl, 8), cl), :]

    def stage_a_copy(t):
        return pltpu.make_async_remote_copy(
            src_ref=send_a.at[t], dst_ref=recv_a.at[t], send_sem=sa.at[t], recv_sem=ra.at[t],
            device_id={"wide": partner}, device_id_type=MESH)

    def stage_b_copies(t):
        return [pltpu.make_async_remote_copy(
            src_ref=send_b.at[t, lax.rem(chip + d, pairs)], dst_ref=recv_b.at[t, d - 1],
            send_sem=sb.at[t, d - 1], recv_sem=rb.at[t, d - 1],
            device_id={"wide": 2 * lax.rem(chip + d, pairs) + core}, device_id_type=MESH)
            for d in range(1, pairs)]

    def stage_c_copy(t):
        return pltpu.make_async_remote_copy(
            src_ref=send_c.at[t], dst_ref=recv_c.at[m], send_sem=sc.at[t], recv_sem=rc.at[m],
            device_id={"narrow": blocks[t]}, device_id_type=MESH)

    def packed(j):
        tiles = [acc[n, pl.ds(j, bl, stride=jt), :] for n in range(acc.shape[0])]
        value = jnp.concatenate(tiles, axis=1)[:, :al]
        return jnp.concatenate([value[q * quarter:(q + 1) * quarter] for q in range(4)], axis=1)

    def compute(t):
        block = blocks[t]
        if t:
            send_left(block).wait_recv()

            @pl.when((block < m) & (m < nn - 1))
            def _():
                send_right(block).start()

            @pl.when((block > m) & (m > 0))
            def _():
                send_left(block).start()

            for r in range(ranks):
                yr[r] = yb[block, :, r * al:(r + 1) * al]
        pair = c_labels ^ iv_row[block]
        for k in range(kt):
            value = jnp.where(pair == (label_i ^ labels[k]), yr[rank_of[k]], 0.0)
            high = value.astype(BF16)
            xh[k * cl:(k + 1) * cl, :al] = high
            xl[k * cl:(k + 1) * cl, :al] = (value - high.astype(F32)).astype(BF16)

        @pl.loop(0, bj // 256)
        def _(tile):
            rows = pl.ds(pl.multiple_of(tile * 256, 256), 256)
            one = jnp.dot(cth[rows, :], xh[...], preferred_element_type=F32)
            two = jnp.dot(cth[rows, :], xl[...], preferred_element_type=F32)
            three = jnp.dot(ctl[rows, :], xh[...], preferred_element_type=F32)
            summed = one + (two + three)
            for n in range(acc.shape[0]):
                acc[n, rows, :] = summed[:, n * 128:(n + 1) * 128]

        for p in range(pairs):
            send_a[t, p] = packed(2 * p + 1 - core)
            send_b[t, p] = packed(2 * p + core)
        stage_a_copy(t).start()

    def finish_a(t):
        stage_a_copy(t).wait()
        for p in range(pairs):
            send_b[t, p] = send_b[t, p] + recv_a[t, p]
        for copy in stage_b_copies(t):
            copy.start()

    def finish_b(t):
        for copy in stage_b_copies(t):
            copy.wait()
        total = send_b[t, chip]
        for d in range(1, pairs):
            total = total + recv_b[t, d - 1]
        if t == 0:
            recv_c[m] = total
        else:
            send_c[t] = total
            stage_c_copy(t).start()

    for t in range(nn):
        compute(t)
        if t >= 1:
            finish_a(t - 1)
        if t >= 2:
            finish_b(t - 2)
    finish_a(nn - 1)
    finish_b(nn - 2)
    finish_b(nn - 1)

    for t in range(1, nn):
        pltpu.make_async_remote_copy(
            src_ref=send_c.at[t], dst_ref=recv_c.at[blocks[t]], send_sem=sc.at[t], recv_sem=rc.at[blocks[t]],
            device_id={"narrow": blocks[t]}, device_id_type=MESH).wait()
    for z in range(nn):
        for q in range(4):
            base = z * bl + q * quarter
            out_t[base:base + quarter, :] = recv_c[z, :, q * al:(q + 1) * al]
    kept = jnp.where(ca == (label_i ^ ir_j[w]), out_t[...], 0.0)
    out[...] = jnp.transpose(kept, (1, 0))

    @pl.when(m < nn - 1)
    def _():
        send_right(m).wait_send()

    @pl.when(m > 0)
    def _():
        send_left(m).wait_send()

    for t in range(1, nn):
        block = blocks[t]

        @pl.when((block < m) & (m < nn - 1))
        def _():
            send_right(block).wait_send()

        @pl.when((block > m) & (m > 0))
        def _():
            send_left(block).wait_send()


def packed_path(ranks, ident, amps, cycle, irrep_i, irrep_k, irrep_j, irrep_v):
    wn = lax.axis_size("wide")
    nn = lax.axis_size("narrow")
    _, kl, al, vt = amps.shape
    kt, cl, bj = cycle.shape
    bl = bj // wn
    depth = kt * cl
    pairs = wn // 2
    pack = (bl // 4, 4 * al)
    lanes = -(-al // 128) * 128
    vmem = pl.BlockSpec(memory_space=pltpu.VMEM)
    smem = pl.BlockSpec(memory_space=pltpu.SMEM)
    dma = pltpu.SemaphoreType.DMA
    result = pl.pallas_call(
        functools.partial(cycle_kernel, ranks, wn, nn),
        out_shape=jax.ShapeDtypeStruct((al, vt), F32),
        in_specs=[vmem, pl.BlockSpec(memory_space=pl.ANY), smem, smem, smem, vmem, vmem],
        out_specs=vmem,
        scratch_shapes=[
            pltpu.VMEM((kt, cl, bj), F32),
            pltpu.VMEM((bj, depth), BF16),
            pltpu.VMEM((bj, depth), BF16),
            pltpu.VMEM((vt, kl * al), F32),
            pltpu.VMEM((wn, cl, kl * al), F32),
            pltpu.VMEM((kt, cl, al), F32),
            pltpu.VMEM((nn, cl, ranks * al), F32),
            pltpu.VMEM((ranks, cl, al), F32),
            pltpu.VMEM((depth, lanes), BF16),
            pltpu.VMEM((depth, lanes), BF16),
            pltpu.VMEM((lanes // 128, bj, 128), F32),
            pltpu.VMEM((nn, pairs) + pack, F32),
            pltpu.VMEM((nn, pairs) + pack, F32),
            pltpu.VMEM((nn, pairs) + pack, F32),
            pltpu.VMEM((nn, pairs - 1) + pack, F32),
            pltpu.VMEM((nn,) + pack, F32),
            pltpu.VMEM((nn,) + pack, F32),
            pltpu.VMEM((vt, al), F32),
            dma, dma((wn,)), dma((wn,)), dma((nn,)), dma((nn,)), dma((nn,)),
            dma((nn,)), dma((nn,)), dma((nn, pairs - 1)), dma((nn, pairs - 1)), dma((nn,)), dma((nn,)),
        ],
        compiler_params=pltpu.CompilerParams(
            collective_id=ident, has_side_effects=True, vmem_limit_bytes=56 * 1024 * 1024),
    )(amps[0], cycle, irrep_i, irrep_k, irrep_j,
      irrep_v.reshape(vt, 1), irrep_v.reshape(nn, 1, al))
    return result.reshape(1, 1, al, vt)


def general_path(amps, cycle, irrep_i, irrep_k, irrep_j, irrep_v):
    wide_pos = lax.axis_index("wide")
    narrow_pos = lax.axis_index("narrow")
    wide_count = lax.axis_size("wide")
    narrow_count = lax.axis_size("narrow")
    i_total = amps.shape[0]
    k_local = amps.shape[1]
    a_local = amps.shape[2]
    v_total = amps.shape[3]
    k_total = cycle.shape[0]
    c_local = cycle.shape[1]
    b_local = v_total // narrow_count
    j_total = cycle.shape[2] // b_local
    j_local = j_total // wide_count
    cycle_four = cycle.reshape(k_total, c_local, b_local, j_total)
    k_labels = lax.dynamic_slice_in_dim(irrep_k, wide_pos * k_local, k_local)
    a_labels = lax.dynamic_slice_in_dim(irrep_v, narrow_pos * a_local, a_local)
    allowed_in = (
        irrep_i[:, None, None, None]
        ^ k_labels[None, :, None, None]
        ^ a_labels[None, None, :, None]
        ^ irrep_v[None, None, None, :]
        == 0
    )
    masked = jnp.where(allowed_in, amps, jnp.zeros_like(amps))
    moved = lax.all_to_all(masked, "wide", split_axis=3, concat_axis=1, tiled=True)
    piece = lax.all_gather(moved, "narrow", axis=2, tiled=True)
    part_sum = jnp.einsum("ikac,kcbj->iajb", piece, cycle_four, precision=lax.Precision.HIGHEST)
    terms = part_sum.reshape(piece.shape[0], piece.shape[2], j_total * b_local)
    summed = lax.psum_scatter(terms, "wide", scatter_dimension=2, tiled=True)
    summed_four = summed.reshape(i_total, v_total, j_local, b_local)
    j_labels = lax.dynamic_slice_in_dim(irrep_j, wide_pos * j_local, j_local)
    b_labels = lax.dynamic_slice_in_dim(irrep_v, narrow_pos * b_local, b_local)
    allowed_out = (
        irrep_i[:, None, None, None]
        ^ irrep_v[None, :, None, None]
        ^ j_labels[None, None, :, None]
        ^ b_labels[None, None, None, :]
        == 0
    )
    result = jnp.where(allowed_out, summed_four, jnp.zeros_like(summed_four)).reshape(
        i_total, v_total, j_local * b_local
    )
    returned = lax.all_to_all(result, "narrow", split_axis=1, concat_axis=2, tiled=True)
    spread = returned.reshape(i_total, a_local, narrow_count, j_local, b_local)
    return jnp.transpose(spread, (0, 3, 1, 2, 4)).reshape(i_total, j_local, a_local, v_total)


def per_device(amps, cycle, irrep_i, irrep_k, irrep_j, irrep_v):
    wn = lax.axis_size("wide")
    nn = lax.axis_size("narrow")
    kt, cl, bj = cycle.shape
    bl = amps.shape[3] // nn
    fits = (amps.shape[0] == 1 and bj == bl * wn and wn % 2 == 0 and cl % 16 == 0 and bl % 32 == 0
            and amps.shape[2] % 32 == 0 and bj % 256 == 0 and (kt * cl) % 128 == 0)
    if not fits:
        return general_path(amps, cycle, irrep_i, irrep_k, irrep_j, irrep_v)
    most = jnp.max(jnp.sum((irrep_k[:, None] == irrep_k[None, :]).astype(jnp.int32), axis=0))
    level = (most > 4).astype(jnp.int32) + (most > 8).astype(jnp.int32)
    return lax.switch(
        level,
        [functools.partial(packed_path, 4, 0), functools.partial(packed_path, 8, 1), general_path],
        amps, cycle, irrep_i, irrep_k, irrep_j, irrep_v)


def solution(mesh):
    placed = (P(None, "wide", "narrow", None), P(None, "wide", "narrow"), P(), P(), P(), P())
    return jax.shard_map(
        per_device,
        mesh=mesh,
        in_specs=placed,
        out_specs=P(None, "wide", "narrow", None),
        check_vma=False,
    )
```

```python
import functools

import jax
import jax.numpy as jnp
from jax import lax
from jax.experimental import pallas as pl
from jax.experimental.pallas import tpu as pltpu
from jax.sharding import PartitionSpec as P

F32 = jnp.float32
BF16 = jnp.bfloat16
MESH = pl.DeviceIdType.MESH


def pick(position, table):
    value = jnp.int32(table[0])
    for place in range(1, len(table)):
        value = jnp.where(position == place, jnp.int32(table[place]), value)
    return value


def near_first(count):
    return [sorted(range(count), key=lambda n: (abs(n - m), n)) for m in range(count)]


def run_starts(labels, count):
    steps = count.bit_length()
    starts = []
    for g in range(1, 8):
        low, high = jnp.int32(0), jnp.int32(count)
        for _ in range(steps):
            middle = (low + high) // 2
            below = (labels[jnp.minimum(middle, count - 1)] < g) & (low < high)
            high = jnp.where(below | (low >= high), high, middle)
            low = jnp.where(below, middle + 1, low)
        starts.append(low)
    return starts


def labels_at(starts, places):
    total = jnp.zeros(places.shape, jnp.int32)
    for start in starts:
        total = total + jnp.where(places >= start, 1, 0)
    return total


def cut_rows(cl):
    units = cl // 16
    first = (units + 1) // 2 * 16
    return [(0, first), (first, cl - first)] if first < cl else [(0, cl)]


def halves_of(rows):
    first = (rows // 8 + 1) // 2 * 8
    return [(0, first), (first, rows - first)] if first < rows else [(0, rows)]


def cycle_kernel(ranks, wn, nn, amps, cycle, ir_i, ir_k, ir_j, ir_v, out,
                 cyc, cth, ctl, amt, recv_one, xk, yb, yr, xh, xl, acc, send_a, recv_a, send_b, recv_b,
                 send_c, recv_c, out_t,
                 cyc_sem, s1, r1, sl, sr, ry, sa, ra, sb, rb, sc, rc):
    w = lax.axis_index("wide")
    m = lax.axis_index("narrow")
    kl, al, vt = amps.shape
    kt, cl, bj = cycle.shape
    jt = wn
    bl = bj // jt
    depth = kt * cl
    quarter = bl // 4
    pairs = wn // 2
    core = lax.rem(w, 2)
    chip = w // 2
    partner = w + 1 - 2 * core

    load = pltpu.make_async_copy(cycle, cyc, cyc_sem)
    load.start()

    barrier = pltpu.get_barrier_semaphore()
    for d in range(1, wn):
        pl.semaphore_signal(barrier, inc=1, device_id={"wide": lax.rem(w + d, wn)}, device_id_type=MESH)
    for d in range(1, nn):
        pl.semaphore_signal(barrier, inc=1, device_id={"narrow": lax.rem(m + d, nn)}, device_id_type=MESH)

    label_i = ir_i[0]
    v_starts = run_starts(ir_v, vt)
    a_places = lax.broadcasted_iota(jnp.int32, (1, al), 1)
    ca = (labels_at(v_starts, lax.broadcasted_iota(jnp.int32, (vt, 1), 0))
          ^ labels_at(v_starts, a_places + m * al))
    cuts = cut_rows(cl)
    halves = halves_of(quarter)
    for e in range(kl):
        turned = jnp.transpose(amps[e], (1, 0))
        kept = jnp.where(ca == (label_i ^ ir_k[w * kl + e]), turned, 0.0)
        for peer in range(wn):
            for start, size in cuts:
                half = size // 2
                for h in range(2):
                    here = peer * cl + start + h * half
                    lane = (2 * e + h) * al
                    amt[peer, start // 2:start // 2 + half, lane:lane + al] = kept[here:here + half]

    pl.semaphore_wait(barrier, wn + nn - 2)

    first = []
    for n, (start, size) in enumerate(cuts):
        rows = pl.ds(start // 2, size // 2)
        first.append([])
        for d in range(1, wn):
            peer = lax.rem(w + d, wn)
            copy = pltpu.make_async_remote_copy(
                src_ref=amt.at[peer, rows], dst_ref=recv_one.at[w, rows],
                send_sem=s1.at[n, d], recv_sem=r1.at[n, d], device_id={"wide": peer}, device_id_type=MESH)
            copy.start()
            first[n].append(copy)
    recv_one[w] = amt[w]

    if xh.shape[1] > al:
        xh[:, al:] = jnp.zeros((depth, xh.shape[1] - al), BF16)
        xl[:, al:] = jnp.zeros((depth, xh.shape[1] - al), BF16)
    load.wait()
    cyc_rows = cyc.reshape(depth, bj)

    @pl.loop(0, depth // 128)
    def _(row):
        here = pl.multiple_of(row * 128, 128)
        for col in range(bj // 128):
            block = jnp.transpose(cyc_rows[pl.ds(here, 128), col * 128:(col + 1) * 128], (1, 0))
            high = block.astype(BF16)
            cth[col * 128:(col + 1) * 128, pl.ds(here, 128)] = high
            ctl[col * 128:(col + 1) * 128, pl.ds(here, 128)] = (block - high.astype(F32)).astype(BF16)

    starts, counts = [], []
    labels = [ir_k[k] for k in range(kt)]
    for g in range(8):
        below = jnp.int32(0)
        same = jnp.int32(0)
        for k in range(kt):
            below = below + jnp.where(labels[k] < g, 1, 0)
            same = same + jnp.where(labels[k] == g, 1, 0)
        starts.append(below)
        counts.append(same)
    rank_of = []
    for k in range(kt):
        place = jnp.int32(0)
        for other in range(k):
            place = place + jnp.where(labels[other] == labels[k], 1, 0)
        rank_of.append(jnp.minimum(place, ranks - 1))

    def send_right(block, n):
        rows = pl.ds(*cuts[n])
        return pltpu.make_async_remote_copy(
            src_ref=yb.at[block, rows], dst_ref=yb.at[block, rows], send_sem=sr.at[block, n],
            recv_sem=ry.at[block, n], device_id={"narrow": jnp.minimum(m + 1, nn - 1)}, device_id_type=MESH)

    def send_left(block, n):
        rows = pl.ds(*cuts[n])
        return pltpu.make_async_remote_copy(
            src_ref=yb.at[block, rows], dst_ref=yb.at[block, rows], send_sem=sl.at[block, n],
            recv_sem=ry.at[block, n], device_id={"narrow": jnp.maximum(m - 1, 0)}, device_id_type=MESH)

    for n, (start, size) in enumerate(cuts):
        for copy in first[n]:
            copy.wait()
        half = size // 2
        for src in range(wn):
            for e in range(kl):
                for h in range(2):
                    lane = (2 * e + h) * al
                    xk[src * kl + e, start + h * half:start + (h + 1) * half] = (
                        recv_one[src, start // 2:start // 2 + half, lane:lane + al])
        for r in range(ranks):
            total = jnp.zeros((size, al), F32)
            for g in range(8):
                value = xk[jnp.minimum(starts[g] + r, kt - 1), start:start + size]
                total = total + jnp.where(r < counts[g], value, 0.0)
            yr[r, start:start + size] = total
        yb[m, start:start + size] = jnp.concatenate([yr[r, start:start + size] for r in range(ranks)], axis=1)

        @pl.when(m < nn - 1)
        def _():
            send_right(m, n).start()

        @pl.when(m > 0)
        def _():
            send_left(m, n).start()

    order = near_first(nn)
    blocks = [pick(m, [order[z][t] for z in range(nn)]) for t in range(nn)]
    c_labels = labels_at(v_starts, lax.broadcasted_iota(jnp.int32, (cl, 1), 0) + w * cl)

    def stage_a_copy(t, h):
        return pltpu.make_async_remote_copy(
            src_ref=send_a.at[t, h, :, pl.ds(0, halves[h][1])], dst_ref=recv_a.at[t, h, :, pl.ds(0, halves[h][1])],
            send_sem=sa.at[t, h], recv_sem=ra.at[t, h],
            device_id={"wide": partner}, device_id_type=MESH)

    def stage_b_copies(t, h):
        rows = pl.ds(*halves[h])
        return [pltpu.make_async_remote_copy(
            src_ref=send_b.at[t, lax.rem(chip + d, pairs), rows], dst_ref=recv_b.at[t, d - 1, rows],
            send_sem=sb.at[t, h, d - 1], recv_sem=rb.at[t, h, d - 1],
            device_id={"wide": 2 * lax.rem(chip + d, pairs) + core}, device_id_type=MESH)
            for d in range(1, pairs)]

    def stage_c_copy(t, h, slot):
        rows = pl.ds(*halves[h])
        return pltpu.make_async_remote_copy(
            src_ref=send_c.at[t, rows], dst_ref=recv_c.at[slot, rows], send_sem=sc.at[t, h],
            recv_sem=rc.at[slot, h], device_id={"narrow": blocks[t]}, device_id_type=MESH)

    def packed(j):
        tiles = [acc[n, pl.ds(j, bl, stride=jt), :] for n in range(acc.shape[0])]
        value = jnp.concatenate(tiles, axis=1)[:, :al]
        return jnp.concatenate([value[q * quarter:(q + 1) * quarter] for q in range(4)], axis=1)

    def compute(t):
        block = blocks[t]
        if t:
            for n in range(len(cuts)):
                send_left(block, n).wait_recv()

                @pl.when((block < m) & (m < nn - 1))
                def _():
                    send_right(block, n).start()

                @pl.when((block > m) & (m > 0))
                def _():
                    send_left(block, n).start()

            for r in range(ranks):
                yr[r] = yb[block, :, r * al:(r + 1) * al]
        pair = c_labels ^ labels_at(v_starts, a_places + block * al)
        for k in range(kt):
            value = jnp.where(pair == (label_i ^ labels[k]), yr[rank_of[k]], 0.0)
            high = value.astype(BF16)
            xh[k * cl:(k + 1) * cl, :al] = high
            xl[k * cl:(k + 1) * cl, :al] = (value - high.astype(F32)).astype(BF16)

        @pl.loop(0, bj // 256)
        def _(tile):
            rows = pl.ds(pl.multiple_of(tile * 256, 256), 256)
            one = jnp.dot(cth[rows, :], xh[...], preferred_element_type=F32)
            two = jnp.dot(cth[rows, :], xl[...], preferred_element_type=F32)
            three = jnp.dot(ctl[rows, :], xh[...], preferred_element_type=F32)
            summed = one + (two + three)
            for n in range(acc.shape[0]):
                acc[n, rows, :] = summed[:, n * 128:(n + 1) * 128]

        for p in range(pairs):
            value = packed(2 * p + 1 - core)
            for h, (start, size) in enumerate(halves):
                send_a[t, h, p, :size] = value[start:start + size]
        for h in range(len(halves)):
            stage_a_copy(t, h).start()
        for p in range(pairs):
            send_b[t, p] = packed(2 * p + core)

    def finish_a(t, h):
        start, size = halves[h]
        stage_a_copy(t, h).wait()
        for p in range(pairs):
            send_b[t, p, start:start + size] = send_b[t, p, start:start + size] + recv_a[t, h, p, :size]
        for copy in stage_b_copies(t, h):
            copy.start()

    def finish_b(t, h):
        start, size = halves[h]
        for copy in stage_b_copies(t, h):
            copy.wait()
        total = send_b[t, chip, start:start + size]
        for d in range(1, pairs):
            total = total + recv_b[t, d - 1, start:start + size]
        if t == 0:
            recv_c[m, start:start + size] = total
        else:
            send_c[t, start:start + size] = total
            stage_c_copy(t, h, m).start()

    for t in range(nn):
        compute(t)
        for h in range(len(halves)):
            if t >= 1:
                finish_a(t - 1, h)
        for h in range(len(halves)):
            if t >= 2:
                finish_b(t - 2, h)
    for h in range(len(halves)):
        finish_a(nn - 1, h)
    for h in range(len(halves)):
        finish_b(nn - 2, h)
    for h in range(len(halves)):
        finish_b(nn - 1, h)

    for t in range(1, nn):
        for h in range(len(halves)):
            stage_c_copy(t, h, blocks[t]).wait()
    for z in range(nn):
        for q in range(4):
            base = z * bl + q * quarter
            out_t[base:base + quarter, :] = recv_c[z, :, q * al:(q + 1) * al]
    kept = jnp.where(ca == (label_i ^ ir_j[w]), out_t[...], 0.0)
    out[...] = jnp.transpose(kept, (1, 0))

    for n in range(len(cuts)):
        @pl.when(m < nn - 1)
        def _():
            send_right(m, n).wait_send()

        @pl.when(m > 0)
        def _():
            send_left(m, n).wait_send()

        for t in range(1, nn):
            block = blocks[t]

            @pl.when((block < m) & (m < nn - 1))
            def _():
                send_right(block, n).wait_send()

            @pl.when((block > m) & (m > 0))
            def _():
                send_left(block, n).wait_send()


def packed_path(ranks, ident, amps, cycle, irrep_i, irrep_k, irrep_j, irrep_v):
    wn = lax.axis_size("wide")
    nn = lax.axis_size("narrow")
    _, kl, al, vt = amps.shape
    kt, cl, bj = cycle.shape
    bl = bj // wn
    depth = kt * cl
    pairs = wn // 2
    pack = (bl // 4, 4 * al)
    lanes = -(-al // 128) * 128
    cn = len(cut_rows(cl))
    hn = len(halves_of(bl // 4))
    most = halves_of(bl // 4)[0][1]
    vmem = pl.BlockSpec(memory_space=pltpu.VMEM)
    smem = pl.BlockSpec(memory_space=pltpu.SMEM)
    dma = pltpu.SemaphoreType.DMA
    result = pl.pallas_call(
        functools.partial(cycle_kernel, ranks, wn, nn),
        out_shape=jax.ShapeDtypeStruct((al, vt), F32),
        in_specs=[vmem, pl.BlockSpec(memory_space=pl.ANY), smem, smem, smem, smem],
        out_specs=vmem,
        scratch_shapes=[
            pltpu.VMEM((kt, cl, bj), F32),
            pltpu.VMEM((bj, depth), BF16),
            pltpu.VMEM((bj, depth), BF16),
            pltpu.VMEM((wn, cl // 2, 2 * kl * al), F32),
            pltpu.VMEM((wn, cl // 2, 2 * kl * al), F32),
            pltpu.VMEM((kt, cl, al), F32),
            pltpu.VMEM((nn, cl, ranks * al), F32),
            pltpu.VMEM((ranks, cl, al), F32),
            pltpu.VMEM((depth, lanes), BF16),
            pltpu.VMEM((depth, lanes), BF16),
            pltpu.VMEM((lanes // 128, bj, 128), F32),
            pltpu.VMEM((nn, hn, pairs, most, 4 * al), F32),
            pltpu.VMEM((nn, hn, pairs, most, 4 * al), F32),
            pltpu.VMEM((nn, pairs) + pack, F32),
            pltpu.VMEM((nn, pairs - 1) + pack, F32),
            pltpu.VMEM((nn,) + pack, F32),
            pltpu.VMEM((nn,) + pack, F32),
            pltpu.VMEM((vt, al), F32),
            dma, dma((cn, wn)), dma((cn, wn)), dma((nn, cn)), dma((nn, cn)), dma((nn, cn)),
            dma((nn, hn)), dma((nn, hn)), dma((nn, hn, pairs - 1)), dma((nn, hn, pairs - 1)),
            dma((nn, hn)), dma((nn, hn)),
        ],
        compiler_params=pltpu.CompilerParams(
            collective_id=ident, has_side_effects=True, vmem_limit_bytes=56 * 1024 * 1024),
    )(amps[0], cycle, irrep_i, irrep_k, irrep_j, irrep_v)
    return result.reshape(1, 1, al, vt)


def general_path(amps, cycle, irrep_i, irrep_k, irrep_j, irrep_v):
    wide_pos = lax.axis_index("wide")
    narrow_pos = lax.axis_index("narrow")
    wide_count = lax.axis_size("wide")
    narrow_count = lax.axis_size("narrow")
    i_total = amps.shape[0]
    k_local = amps.shape[1]
    a_local = amps.shape[2]
    v_total = amps.shape[3]
    k_total = cycle.shape[0]
    c_local = cycle.shape[1]
    b_local = v_total // narrow_count
    j_total = cycle.shape[2] // b_local
    j_local = j_total // wide_count
    cycle_four = cycle.reshape(k_total, c_local, b_local, j_total)
    k_labels = lax.dynamic_slice_in_dim(irrep_k, wide_pos * k_local, k_local)
    a_labels = lax.dynamic_slice_in_dim(irrep_v, narrow_pos * a_local, a_local)
    allowed_in = (
        irrep_i[:, None, None, None]
        ^ k_labels[None, :, None, None]
        ^ a_labels[None, None, :, None]
        ^ irrep_v[None, None, None, :]
        == 0
    )
    masked = jnp.where(allowed_in, amps, jnp.zeros_like(amps))
    moved = lax.all_to_all(masked, "wide", split_axis=3, concat_axis=1, tiled=True)
    piece = lax.all_gather(moved, "narrow", axis=2, tiled=True)
    part_sum = jnp.einsum("ikac,kcbj->iajb", piece, cycle_four, precision=lax.Precision.HIGHEST)
    terms = part_sum.reshape(piece.shape[0], piece.shape[2], j_total * b_local)
    summed = lax.psum_scatter(terms, "wide", scatter_dimension=2, tiled=True)
    summed_four = summed.reshape(i_total, v_total, j_local, b_local)
    j_labels = lax.dynamic_slice_in_dim(irrep_j, wide_pos * j_local, j_local)
    b_labels = lax.dynamic_slice_in_dim(irrep_v, narrow_pos * b_local, b_local)
    allowed_out = (
        irrep_i[:, None, None, None]
        ^ irrep_v[None, :, None, None]
        ^ j_labels[None, None, :, None]
        ^ b_labels[None, None, None, :]
        == 0
    )
    result = jnp.where(allowed_out, summed_four, jnp.zeros_like(summed_four)).reshape(
        i_total, v_total, j_local * b_local
    )
    returned = lax.all_to_all(result, "narrow", split_axis=1, concat_axis=2, tiled=True)
    spread = returned.reshape(i_total, a_local, narrow_count, j_local, b_local)
    return jnp.transpose(spread, (0, 3, 1, 2, 4)).reshape(i_total, j_local, a_local, v_total)


def per_device(amps, cycle, irrep_i, irrep_k, irrep_j, irrep_v):
    wn = lax.axis_size("wide")
    nn = lax.axis_size("narrow")
    kt, cl, bj = cycle.shape
    bl = amps.shape[3] // nn
    fits = (amps.shape[0] == 1 and bj == bl * wn and wn % 2 == 0 and cl % 16 == 0 and bl % 32 == 0
            and amps.shape[2] % 32 == 0 and bj % 256 == 0 and (kt * cl) % 128 == 0)
    if not fits:
        return general_path(amps, cycle, irrep_i, irrep_k, irrep_j, irrep_v)
    apart = jnp.arange(kt)
    over_4 = (irrep_k == jnp.roll(irrep_k, 4)) & (apart >= 4)
    over_8 = (irrep_k == jnp.roll(irrep_k, 8)) & (apart >= 8)
    level = jnp.max(over_4.astype(jnp.int32) + over_8.astype(jnp.int32))
    return lax.switch(
        level,
        [functools.partial(packed_path, 4, 0), functools.partial(packed_path, 8, 1), general_path],
        amps, cycle, irrep_i, irrep_k, irrep_j, irrep_v)


def solution(mesh):
    placed = (P(None, "wide", "narrow", None), P(None, "wide", "narrow"), P(), P(), P(), P())
    return jax.shard_map(
        per_device,
        mesh=mesh,
        in_specs=placed,
        out_specs=P(None, "wide", "narrow", None),
        check_vma=False,
    )
```

```python
import functools

import jax
import jax.numpy as jnp
from jax import lax
from jax.experimental import pallas as pl
from jax.experimental.pallas import tpu as pltpu
from jax.sharding import PartitionSpec as P

F32 = jnp.float32
BF16 = jnp.bfloat16
MESH = pl.DeviceIdType.MESH
TILE = 640
LEVELS = (4, 6, 8)


def pick(position, table):
    value = jnp.int32(table[0])
    for place in range(1, len(table)):
        value = jnp.where(position == place, jnp.int32(table[place]), value)
    return value


def near_first(count):
    return [sorted(range(count), key=lambda n: (abs(n - m), n)) for m in range(count)]


def run_starts(labels, count):
    steps = count.bit_length()
    starts = []
    for g in range(1, 8):
        low, high = jnp.int32(0), jnp.int32(count)
        for _ in range(steps):
            middle = (low + high) // 2
            below = (labels[jnp.minimum(middle, count - 1)] < g) & (low < high)
            high = jnp.where(below | (low >= high), high, middle)
            low = jnp.where(below, middle + 1, low)
        starts.append(low)
    return starts


def labels_at(starts, places):
    total = jnp.zeros(places.shape, jnp.int32)
    for start in starts:
        total = total + jnp.where(places >= start, 1, 0)
    return total


def cut_rows(cl):
    units = cl // 16
    first = (units + 1) // 2 * 16
    return [(0, first), (first, cl - first)] if first < cl else [(0, cl)]


def halves_of(rows):
    first = (rows // 8 + 1) // 2 * 8
    return [(0, first), (first, rows - first)] if first < rows else [(0, rows)]


def cycle_kernel(ranks, wn, nn, amps, cycle, ir_i, ir_k, ir_j, ir_v, out,
                 cyc, cth, ctl, amt, recv_one, xk, yb, yr, xh, xl, acc, send_a, recv_a, send_b, recv_b,
                 send_c, recv_c, out_t,
                 cyc_sem, s1, r1, sl, sr, ry, sa, ra, sb, rb, sc, rc):
    w = lax.axis_index("wide")
    m = lax.axis_index("narrow")
    kl, al, vt = amps.shape
    kt, cl, bj = cycle.shape
    jt = wn
    bl = bj // jt
    depth = kt * cl
    quarter = bl // 4
    pairs = wn // 2
    core = lax.rem(w, 2)
    chip = w // 2
    partner = w + 1 - 2 * core

    load = pltpu.make_async_copy(cycle, cyc, cyc_sem)
    load.start()

    barrier = pltpu.get_barrier_semaphore()
    for d in range(1, wn):
        pl.semaphore_signal(barrier, inc=1, device_id={"wide": lax.rem(w + d, wn)}, device_id_type=MESH)
    for d in range(1, nn):
        pl.semaphore_signal(barrier, inc=1, device_id={"narrow": lax.rem(m + d, nn)}, device_id_type=MESH)

    label_i = ir_i[0]
    v_starts = run_starts(ir_v, vt)
    a_places = lax.broadcasted_iota(jnp.int32, (1, al), 1)
    ca = (labels_at(v_starts, lax.broadcasted_iota(jnp.int32, (vt, 1), 0))
          ^ labels_at(v_starts, a_places + m * al))
    cuts = cut_rows(cl)
    halves = halves_of(quarter)
    for e in range(kl):
        turned = jnp.transpose(amps[e], (1, 0))
        kept = jnp.where(ca == (label_i ^ ir_k[w * kl + e]), turned, 0.0)
        for peer in range(wn):
            for start, size in cuts:
                half = size // 2
                for h in range(2):
                    here = peer * cl + start + h * half
                    lane = (2 * e + h) * al
                    amt[peer, start // 2:start // 2 + half, lane:lane + al] = kept[here:here + half]

    pl.semaphore_wait(barrier, wn + nn - 2)

    first = []
    for n, (start, size) in enumerate(cuts):
        rows = pl.ds(start // 2, size // 2)
        first.append([])
        for d in range(1, wn):
            peer = lax.rem(w + d, wn)
            copy = pltpu.make_async_remote_copy(
                src_ref=amt.at[peer, rows], dst_ref=recv_one.at[w, rows],
                send_sem=s1.at[n, d], recv_sem=r1.at[n, d], device_id={"wide": peer}, device_id_type=MESH)
            copy.start()
            first[n].append(copy)
    recv_one[w] = amt[w]

    if xh.shape[1] > al:
        xh[:, al:] = jnp.zeros((depth, xh.shape[1] - al), BF16)
        xl[:, al:] = jnp.zeros((depth, xh.shape[1] - al), BF16)
    load.wait()
    cyc_rows = cyc.reshape(depth, bj)

    @pl.loop(0, depth // 128)
    def _(row):
        here = pl.multiple_of(row * 128, 128)
        for col in range(bj // 128):
            block = jnp.transpose(cyc_rows[pl.ds(here, 128), col * 128:(col + 1) * 128], (1, 0))
            high = block.astype(BF16)
            cth[col * 128:(col + 1) * 128, pl.ds(here, 128)] = high
            ctl[col * 128:(col + 1) * 128, pl.ds(here, 128)] = (block - high.astype(F32)).astype(BF16)

    starts, counts = [], []
    labels = [ir_k[k] for k in range(kt)]
    for g in range(8):
        below = jnp.int32(0)
        same = jnp.int32(0)
        for k in range(kt):
            below = below + jnp.where(labels[k] < g, 1, 0)
            same = same + jnp.where(labels[k] == g, 1, 0)
        starts.append(below)
        counts.append(same)
    rank_of = []
    for k in range(kt):
        place = jnp.int32(0)
        for other in range(k):
            place = place + jnp.where(labels[other] == labels[k], 1, 0)
        rank_of.append(jnp.minimum(place, ranks - 1))

    def send_right(block, n):
        rows = pl.ds(*cuts[n])
        return pltpu.make_async_remote_copy(
            src_ref=yb.at[block, rows], dst_ref=yb.at[block, rows], send_sem=sr.at[block, n],
            recv_sem=ry.at[block, n], device_id={"narrow": jnp.minimum(m + 1, nn - 1)}, device_id_type=MESH)

    def send_left(block, n):
        rows = pl.ds(*cuts[n])
        return pltpu.make_async_remote_copy(
            src_ref=yb.at[block, rows], dst_ref=yb.at[block, rows], send_sem=sl.at[block, n],
            recv_sem=ry.at[block, n], device_id={"narrow": jnp.maximum(m - 1, 0)}, device_id_type=MESH)

    for n, (start, size) in enumerate(cuts):
        for copy in first[n]:
            copy.wait()
        half = size // 2
        for src in range(wn):
            for e in range(kl):
                for h in range(2):
                    lane = (2 * e + h) * al
                    xk[src * kl + e, start + h * half:start + (h + 1) * half] = (
                        recv_one[src, start // 2:start // 2 + half, lane:lane + al])
        for r in range(ranks):
            total = jnp.zeros((size, al), F32)
            for g in range(8):
                value = xk[jnp.minimum(starts[g] + r, kt - 1), start:start + size]
                total = total + jnp.where(r < counts[g], value, 0.0)
            yr[r, start:start + size] = total
        yb[m, start:start + size] = jnp.concatenate([yr[r, start:start + size] for r in range(ranks)], axis=1)

        @pl.when(m < nn - 1)
        def _():
            send_right(m, n).start()

        @pl.when(m > 0)
        def _():
            send_left(m, n).start()

    order = near_first(nn)
    flat = [order[z][t] for z in range(nn) for t in range(nn)]

    def block_at(t):
        return pick(m * nn + t, flat)

    c_labels = labels_at(v_starts, lax.broadcasted_iota(jnp.int32, (cl, 1), 0) + w * cl)

    def stage_a_copy(t, h):
        return pltpu.make_async_remote_copy(
            src_ref=send_a.at[t, h, :, pl.ds(0, halves[h][1])], dst_ref=recv_a.at[t, h, :, pl.ds(0, halves[h][1])],
            send_sem=sa.at[t, h], recv_sem=ra.at[t, h],
            device_id={"wide": partner}, device_id_type=MESH)

    def stage_b_copies(t, h):
        rows = pl.ds(*halves[h])
        return [pltpu.make_async_remote_copy(
            src_ref=send_b.at[t, lax.rem(chip + d, pairs), rows], dst_ref=recv_b.at[t, d - 1, rows],
            send_sem=sb.at[t, h, d - 1], recv_sem=rb.at[t, h, d - 1],
            device_id={"wide": 2 * lax.rem(chip + d, pairs) + core}, device_id_type=MESH)
            for d in range(1, pairs)]

    def stage_c_copy(t, h, slot):
        rows = pl.ds(*halves[h])
        return pltpu.make_async_remote_copy(
            src_ref=send_c.at[t, rows], dst_ref=recv_c.at[slot, rows], send_sem=sc.at[t, h],
            recv_sem=rc.at[slot, h], device_id={"narrow": block_at(t)}, device_id_type=MESH)

    def packed(j):
        tiles = [acc[n, pl.ds(j, bl, stride=jt), :] for n in range(acc.shape[0])]
        value = jnp.concatenate(tiles, axis=1)[:, :al]
        return jnp.concatenate([value[q * quarter:(q + 1) * quarter] for q in range(4)], axis=1)

    def compute(t):
        block = block_at(t)

        @pl.when(t > 0)
        def _():
            for n in range(len(cuts)):
                send_left(block, n).wait_recv()

                @pl.when((block < m) & (m < nn - 1))
                def _():
                    send_right(block, n).start()

                @pl.when((block > m) & (m > 0))
                def _():
                    send_left(block, n).start()

            for r in range(ranks):
                yr[r] = yb[block, :, r * al:(r + 1) * al]
        pair = c_labels ^ labels_at(v_starts, a_places + block * al)
        for k in range(kt):
            value = jnp.where(pair == (label_i ^ labels[k]), yr[rank_of[k]], 0.0)
            high = value.astype(BF16)
            xh[k * cl:(k + 1) * cl, :al] = high
            xl[k * cl:(k + 1) * cl, :al] = (value - high.astype(F32)).astype(BF16)

        @pl.loop(0, bj // TILE)
        def _(tile):
            rows = pl.ds(pl.multiple_of(tile * TILE, TILE), TILE)
            one = jnp.dot(cth[rows, :], xh[...], preferred_element_type=F32)
            two = jnp.dot(cth[rows, :], xl[...], preferred_element_type=F32)
            three = jnp.dot(ctl[rows, :], xh[...], preferred_element_type=F32)
            summed = one + (two + three)
            for n in range(acc.shape[0]):
                acc[n, rows, :] = summed[:, n * 128:(n + 1) * 128]

        for p in range(pairs):
            value = packed(2 * p + 1 - core)
            for h, (start, size) in enumerate(halves):
                send_a[t, h, p, :size] = value[start:start + size]
        for h in range(len(halves)):
            stage_a_copy(t, h).start()
        for p in range(pairs):
            send_b[t, p] = packed(2 * p + core)

    def finish_a(t, h):
        start, size = halves[h]
        stage_a_copy(t, h).wait()
        for p in range(pairs):
            send_b[t, p, start:start + size] = send_b[t, p, start:start + size] + recv_a[t, h, p, :size]
        for copy in stage_b_copies(t, h):
            copy.start()

    def finish_b(t, h):
        start, size = halves[h]
        for copy in stage_b_copies(t, h):
            copy.wait()
        total = send_b[t, chip, start:start + size]
        for d in range(1, pairs):
            total = total + recv_b[t, d - 1, start:start + size]

        @pl.when(t == 0)
        def _():
            recv_c[m, start:start + size] = total

        @pl.when(t > 0)
        def _():
            send_c[t, start:start + size] = total
            stage_c_copy(t, h, m).start()

    @pl.loop(0, nn + 2)
    def _(t):
        @pl.when(t < nn)
        def _():
            compute(t)

        @pl.when((t >= 1) & (t <= nn))
        def _():
            for h in range(len(halves)):
                finish_a(t - 1, h)

        @pl.when(t >= 2)
        def _():
            for h in range(len(halves)):
                finish_b(t - 2, h)

    for t in range(1, nn):
        for h in range(len(halves)):
            stage_c_copy(t, h, block_at(t)).wait()
    for z in range(nn):
        for q in range(4):
            base = z * bl + q * quarter
            out_t[base:base + quarter, :] = recv_c[z, :, q * al:(q + 1) * al]
    kept = jnp.where(ca == (label_i ^ ir_j[w]), out_t[...], 0.0)
    out[...] = jnp.transpose(kept, (1, 0))

    for n in range(len(cuts)):
        @pl.when(m < nn - 1)
        def _():
            send_right(m, n).wait_send()

        @pl.when(m > 0)
        def _():
            send_left(m, n).wait_send()

        for t in range(1, nn):
            block = block_at(t)

            @pl.when((block < m) & (m < nn - 1))
            def _():
                send_right(block, n).wait_send()

            @pl.when((block > m) & (m > 0))
            def _():
                send_left(block, n).wait_send()


def packed_path(ranks, ident, amps, cycle, irrep_i, irrep_k, irrep_j, irrep_v):
    wn = lax.axis_size("wide")
    nn = lax.axis_size("narrow")
    _, kl, al, vt = amps.shape
    kt, cl, bj = cycle.shape
    bl = bj // wn
    depth = kt * cl
    pairs = wn // 2
    pack = (bl // 4, 4 * al)
    lanes = -(-al // 128) * 128
    cn = len(cut_rows(cl))
    hn = len(halves_of(bl // 4))
    most = halves_of(bl // 4)[0][1]
    vmem = pl.BlockSpec(memory_space=pltpu.VMEM)
    smem = pl.BlockSpec(memory_space=pltpu.SMEM)
    dma = pltpu.SemaphoreType.DMA
    result = pl.pallas_call(
        functools.partial(cycle_kernel, ranks, wn, nn),
        out_shape=jax.ShapeDtypeStruct((al, vt), F32),
        in_specs=[vmem, pl.BlockSpec(memory_space=pl.ANY), smem, smem, smem, smem],
        out_specs=vmem,
        scratch_shapes=[
            pltpu.VMEM((kt, cl, bj), F32),
            pltpu.VMEM((bj, depth), BF16),
            pltpu.VMEM((bj, depth), BF16),
            pltpu.VMEM((wn, cl // 2, 2 * kl * al), F32),
            pltpu.VMEM((wn, cl // 2, 2 * kl * al), F32),
            pltpu.VMEM((kt, cl, al), F32),
            pltpu.VMEM((nn, cl, ranks * al), F32),
            pltpu.VMEM((ranks, cl, al), F32),
            pltpu.VMEM((depth, lanes), BF16),
            pltpu.VMEM((depth, lanes), BF16),
            pltpu.VMEM((lanes // 128, bj, 128), F32),
            pltpu.VMEM((nn, hn, pairs, most, 4 * al), F32),
            pltpu.VMEM((nn, hn, pairs, most, 4 * al), F32),
            pltpu.VMEM((nn, pairs) + pack, F32),
            pltpu.VMEM((nn, pairs - 1) + pack, F32),
            pltpu.VMEM((nn,) + pack, F32),
            pltpu.VMEM((nn,) + pack, F32),
            pltpu.VMEM((vt, al), F32),
            dma, dma((cn, wn)), dma((cn, wn)), dma((nn, cn)), dma((nn, cn)), dma((nn, cn)),
            dma((nn, hn)), dma((nn, hn)), dma((nn, hn, pairs - 1)), dma((nn, hn, pairs - 1)),
            dma((nn, hn)), dma((nn, hn)),
        ],
        compiler_params=pltpu.CompilerParams(
            collective_id=ident, has_side_effects=True, vmem_limit_bytes=56 * 1024 * 1024),
    )(amps[0], cycle, irrep_i, irrep_k, irrep_j, irrep_v)
    return result.reshape(1, 1, al, vt)


def general_path(amps, cycle, irrep_i, irrep_k, irrep_j, irrep_v):
    wide_pos = lax.axis_index("wide")
    narrow_pos = lax.axis_index("narrow")
    wide_count = lax.axis_size("wide")
    narrow_count = lax.axis_size("narrow")
    i_total = amps.shape[0]
    k_local = amps.shape[1]
    a_local = amps.shape[2]
    v_total = amps.shape[3]
    k_total = cycle.shape[0]
    c_local = cycle.shape[1]
    b_local = v_total // narrow_count
    j_total = cycle.shape[2] // b_local
    j_local = j_total // wide_count
    cycle_four = cycle.reshape(k_total, c_local, b_local, j_total)
    k_labels = lax.dynamic_slice_in_dim(irrep_k, wide_pos * k_local, k_local)
    a_labels = lax.dynamic_slice_in_dim(irrep_v, narrow_pos * a_local, a_local)
    allowed_in = (
        irrep_i[:, None, None, None]
        ^ k_labels[None, :, None, None]
        ^ a_labels[None, None, :, None]
        ^ irrep_v[None, None, None, :]
        == 0
    )
    masked = jnp.where(allowed_in, amps, jnp.zeros_like(amps))
    moved = lax.all_to_all(masked, "wide", split_axis=3, concat_axis=1, tiled=True)
    piece = lax.all_gather(moved, "narrow", axis=2, tiled=True)
    part_sum = jnp.einsum("ikac,kcbj->iajb", piece, cycle_four, precision=lax.Precision.HIGHEST)
    terms = part_sum.reshape(piece.shape[0], piece.shape[2], j_total * b_local)
    summed = lax.psum_scatter(terms, "wide", scatter_dimension=2, tiled=True)
    summed_four = summed.reshape(i_total, v_total, j_local, b_local)
    j_labels = lax.dynamic_slice_in_dim(irrep_j, wide_pos * j_local, j_local)
    b_labels = lax.dynamic_slice_in_dim(irrep_v, narrow_pos * b_local, b_local)
    allowed_out = (
        irrep_i[:, None, None, None]
        ^ irrep_v[None, :, None, None]
        ^ j_labels[None, None, :, None]
        ^ b_labels[None, None, None, :]
        == 0
    )
    result = jnp.where(allowed_out, summed_four, jnp.zeros_like(summed_four)).reshape(
        i_total, v_total, j_local * b_local
    )
    returned = lax.all_to_all(result, "narrow", split_axis=1, concat_axis=2, tiled=True)
    spread = returned.reshape(i_total, a_local, narrow_count, j_local, b_local)
    return jnp.transpose(spread, (0, 3, 1, 2, 4)).reshape(i_total, j_local, a_local, v_total)


def level_kernel(labels, out):
    count = labels.shape[0]
    level = jnp.int32(0)
    for ranks in LEVELS:
        over = jnp.int32(0)
        for k in range(ranks, count):
            over = over | jnp.where(labels[k] == labels[k - ranks], 1, 0)
        level = level + over
    out[0] = level


def per_device(amps, cycle, irrep_i, irrep_k, irrep_j, irrep_v):
    wn = lax.axis_size("wide")
    nn = lax.axis_size("narrow")
    kt, cl, bj = cycle.shape
    bl = amps.shape[3] // nn
    fits = (amps.shape[0] == 1 and bj == bl * wn and wn % 2 == 0 and cl % 16 == 0 and bl % 32 == 0
            and amps.shape[2] % 32 == 0 and bj % TILE == 0 and (kt * cl) % 128 == 0)
    if not fits:
        return general_path(amps, cycle, irrep_i, irrep_k, irrep_j, irrep_v)
    level = pl.pallas_call(
        level_kernel,
        out_shape=jax.ShapeDtypeStruct((1,), jnp.int32),
        in_specs=[pl.BlockSpec(memory_space=pltpu.SMEM)],
        out_specs=pl.BlockSpec(memory_space=pltpu.SMEM),
    )(irrep_k)[0]
    paths = [functools.partial(packed_path, ranks, n) for n, ranks in enumerate(LEVELS)]
    return lax.switch(
        level, paths + [general_path], amps, cycle, irrep_i, irrep_k, irrep_j, irrep_v)


def solution(mesh):
    placed = (P(None, "wide", "narrow", None), P(None, "wide", "narrow"), P(), P(), P(), P())
    return jax.shard_map(
        per_device,
        mesh=mesh,
        in_specs=placed,
        out_specs=P(None, "wide", "narrow", None),
        check_vma=False,
    )
```
